32 devices in a mesh: dp: 8 (over z, core), mp: 4 (over y, x).
Axes of the slice: x: 2, y: 2, z: 4, core: 2. Of those that a mesh axis runs over, the one named last changes fastest.
Arguments:
- queries: bfloat16 [2048, 4096], P('dp', 'mp'), may hold values from -6 to 6
- keys: bfloat16 [2048, 4096], P('dp', 'mp'), may hold values from -6 to 6
- values: bfloat16 [2048, 4096], P('dp', 'mp'), may hold values from -6 to 6
- query_gain: float32 [128], replicated, may hold values from 0.1 to 1.9
- key_gain: float32 [128], replicated, may hold values from 0.1 to 1.9
- segments: int32 [2048], P('dp'), may hold values from 0 to 7, as said below
- patch_rows: int32 [2048], P('dp'), may hold values from 0 to 62, as said below
- patch_cols: int32 [2048], P('dp'), may hold values from 0 to 15, as said below
- image_counts: int32 [8], P('dp'), may hold values from 7 to 8, as said below
- out_weight: bfloat16 [4096, 3072], P(('mp', 'dp')), may hold values from -0.09375 to 0.09375
- cotangent: bfloat16 [2048, 3072], P(('dp', 'mp')), may hold values from -3 to 3
Outputs:
- projected: bfloat16 [2048, 3072], P(('dp', 'mp'))
- grad_queries: bfloat16 [2048, 4096], P('dp', 'mp')
- grad_keys: bfloat16 [2048, 4096], P('dp', 'mp')
- grad_values: bfloat16 [2048, 4096], P('dp', 'mp')
- grad_weight: float32 [4096, 3072], P(('mp', 'dp'))
The draws below stay inside these ranges and needn't reach their ends.
Inputs may be any that keep to these rules, and one draw needn't show every extreme that they name: `segments`: each sequence of 256 tokens holds 8 images, each a nonempty run of consecutive tokens, numbered 0 to 7 in order. `patch_rows`: patch row of a token within its image: its place in the image divided by the image's patch columns, rounded down. `patch_cols`: patch column of a token within its image: its place in the image modulo the image's patch columns, which are 4 to 16. `image_counts`: a sequence's images with number at least its count are padding.
All inputs are finite; a program needn't handle non-finite values.
Results may differ from the reference program's by a relative error of at most 0.009.
Values may be sent and summed in bfloat16 or wider, within the bound.
A program may use at most 128 MiB of HBM per device.

```python
import math
import jax
import jax.numpy as jnp
from jax import lax

DIM = 3072
HEADS = 32
HD = 128
SEQ = 256
IMAGES = 8
TOKENS = 2048
N_DP = 8
N_MP = 4


def layout(key):
    base = jax.random.fold_in(key, 17)

    def one_sequence(index):
        seq_key = jax.random.fold_in(base, index)
        shuffled = jax.random.permutation(jax.random.fold_in(seq_key, 1), SEQ - 1).astype(jnp.int32)
        random_cuts = jnp.sort(shuffled[:IMAGES - 1] + 1)
        fixed_cuts = SEQ - IMAGES + 1 + jnp.arange(IMAGES - 1, dtype=jnp.int32)
        cut_points = jnp.where(index < 2, fixed_cuts, random_cuts)
        position = jnp.arange(SEQ, dtype=jnp.int32)
        image_id = jnp.sum((position[:, None] >= cut_points[None, :]).astype(jnp.int32), axis=1)
        image_starts = jnp.concatenate([jnp.zeros((1,), jnp.int32), cut_points])
        matches = image_id[:, None] == jnp.arange(IMAGES, dtype=jnp.int32)[None, :]
        start_of = jnp.sum(jnp.where(matches, image_starts[None, :], 0), axis=1)
        drawn_widths = jax.random.randint(jax.random.fold_in(seq_key, 2), (IMAGES,), 4, 17).astype(jnp.int32)
        first_width = jnp.where(index == 0, 4, jnp.where(index == 1, 16, drawn_widths[0])).astype(jnp.int32)
        is_first = jnp.arange(IMAGES, dtype=jnp.int32) == 0
        widths = jnp.where(is_first, first_width, drawn_widths).astype(jnp.int32)
        width_of = jnp.sum(jnp.where(matches, widths[None, :], 0), axis=1)
        local_place = position - start_of
        return (image_id, local_place // width_of, local_place % width_of)
    image_ids, row_ids, col_ids = jax.vmap(one_sequence)(jnp.arange(N_DP, dtype=jnp.int32))
    counts = IMAGES - jax.random.randint(jax.random.fold_in(base, 5), (N_DP,), 0, 2).astype(jnp.int32)
    return (image_ids.reshape(-1), row_ids.reshape(-1), col_ids.reshape(-1), counts)


def draw_segments(key, part):
    return layout(key)[0]


def draw_patch_rows(key, part):
    return layout(key)[1]


def draw_patch_cols(key, part):
    return layout(key)[2]


def draw_image_counts(key, part):
    return layout(key)[3]


def level_of(rng, shape, split, low, largest):
    def one(dim, blocks):
        steps = jax.random.uniform(jax.random.fold_in(jax.random.fold_in(rng, 6), dim), (blocks,), jnp.float32, low / len(split), largest / len(split))
        return jnp.repeat(jnp.exp(steps), shape[dim] // blocks).reshape((-1,) + (1,) * (len(shape) - dim - 1))

    level = one(*split[0])
    for cut in split[1:]:
        level = level * one(*cut)
    return level


def noise(stream_key, extent, scale, reach, cuts=(), held_as=jnp.bfloat16):
    values = jax.random.normal(stream_key, extent, jnp.float32) * scale
    if len(cuts) > 0:
        values = level_of(stream_key, extent, cuts, -0.22, 0.18) * values
    return jnp.clip(values, min=-reach, max=reach).astype(held_as)


def setup_inputs(seed: int = 0) -> dict:
    key_of = jax.random.split(jax.random.key(seed), 12)
    return {
        "queries": noise(key_of[0], (TOKENS, HEADS * HD), 1.0, 6.0, ((0, 8), (1, 4))),
        "keys": noise(key_of[1], (TOKENS, HEADS * HD), 1.0, 6.0, ((0, 8), (1, 4))),
        "values": noise(key_of[2], (TOKENS, HEADS * HD), 1.0, 6.0, ((0, 8), (1, 4))),
        "query_gain": jnp.clip(1.0 + 0.18 * jax.random.normal(key_of[3], (HD,), jnp.float32), 0.1, 1.9),
        "key_gain": jnp.clip(1.0 + 0.18 * jax.random.normal(key_of[4], (HD,), jnp.float32), 0.1, 1.9),
        "segments": draw_segments(jax.random.fold_in(key_of[11], 71), 0),
        "patch_rows": draw_patch_rows(jax.random.fold_in(key_of[11], 71), 0),
        "patch_cols": draw_patch_cols(jax.random.fold_in(key_of[11], 71), 0),
        "image_counts": draw_image_counts(jax.random.fold_in(key_of[11], 71), 0),
        "out_weight": noise(key_of[9], (HEADS * HD, DIM), (HEADS * HD) ** -0.5, 0.09375, ((0, 32),)),
        "cotangent": noise(key_of[10], (TOKENS, DIM), 0.2, 3.0, ((0, 32),)),
    }


def norm_rotate(heads_data, gain, patch_rows, patch_cols):
    center = heads_data - lax.optimization_barrier(jnp.mean(heads_data, axis=-1, keepdims=True))
    spread = lax.optimization_barrier(jnp.mean(center * center, axis=-1, keepdims=True))
    normed = center * lax.rsqrt(spread + 1e-06) * gain
    tokens_here, head_count, head_dim = normed.shape
    quarter = head_dim // 4
    frequency = 10000.0 ** (-jnp.arange(quarter, dtype=jnp.float32) / quarter)
    angles = jnp.stack([patch_rows.astype(jnp.float32)[:, None] * frequency, patch_cols.astype(jnp.float32)[:, None] * frequency], axis=1)
    cosine = jnp.cos(angles)[:, None]
    sine_table = jnp.sin(angles)[:, None]
    grouped = normed.reshape(tokens_here, head_count, 2, 2, quarter)
    lower_part = grouped[:, :, :, 0]
    upper_part = grouped[:, :, :, 1]
    rotated = jnp.stack([lower_part * cosine - upper_part * sine_table, upper_part * cosine + lower_part * sine_table], axis=3)
    return rotated.reshape(tokens_here, head_count, head_dim)

def attend(queries, keys, values, segments, patch_rows, patch_cols, image_count, query_gain, key_gain):
    head_dim = query_gain.shape[0]
    tokens_here = queries.shape[0]
    shaped = (tokens_here, -1, head_dim)
    query_rot = norm_rotate(queries.astype(jnp.float32).reshape(shaped), query_gain, patch_rows, patch_cols)
    key_rot = norm_rotate(keys.astype(jnp.float32).reshape(shaped), key_gain, patch_rows, patch_cols)
    scores = jnp.einsum('shd,thd->hst', query_rot, key_rot, precision=lax.Precision.HIGHEST) / math.sqrt(head_dim)
    allowed = (segments[:, None] == segments[None, :])[None]
    exp_scores = jnp.where(allowed, jnp.exp(scores), 0.0)
    softmax_weights = exp_scores / lax.optimization_barrier(jnp.sum(exp_scores, axis=-1, keepdims=True))
    rounded = lax.optimization_barrier(softmax_weights.astype(jnp.bfloat16)).astype(jnp.float32)
    weights_used = softmax_weights + lax.stop_gradient(rounded - softmax_weights)
    context = jnp.einsum('hst,thd->shd', weights_used, values.astype(jnp.float32).reshape(shaped), precision=lax.Precision.HIGHEST)
    live_rows = (segments < image_count).astype(jnp.float32)
    return (context * live_rows[:, None, None]).reshape(tokens_here, -1).astype(jnp.bfloat16)

def reference(queries, keys, values, query_gain, key_gain, segments, patch_rows, patch_cols, image_counts, out_weight, cotangent):
    group_width = HEADS * HD // N_MP
    weight_groups = out_weight.astype(jnp.float32).reshape(N_MP, group_width, DIM)
    inputs = (queries.reshape(N_DP, SEQ, HEADS * HD), keys.reshape(N_DP, SEQ, HEADS * HD), values.reshape(N_DP, SEQ, HEADS * HD), segments.reshape(N_DP, SEQ), patch_rows.reshape(N_DP, SEQ), patch_cols.reshape(N_DP, SEQ), image_counts, cotangent.reshape(N_DP, SEQ, DIM))

    def per_sequence(grad_sum, sequence_data):
        query_seq, key_seq, value_seq, segment_seq, row_seq, col_seq, image_count, cotangent_seq = sequence_data

        def attention_core(query_part, key_part, value_part):
            return attend(query_part, key_part, value_part, segment_seq, row_seq, col_seq, image_count, query_gain, key_gain)
        attended, pullback = jax.vjp(attention_core, query_seq, key_seq, value_seq)
        attended_groups = attended.astype(jnp.float32).reshape(SEQ, N_MP, group_width)
        group_partial = jnp.einsum('sgc,gcd->gsd', attended_groups, weight_groups, precision=lax.Precision.HIGHEST)
        group_partial = lax.optimization_barrier(group_partial.astype(jnp.bfloat16)).astype(jnp.float32)
        projected = lax.optimization_barrier(jnp.sum(group_partial, axis=0)).astype(jnp.bfloat16)
        d_attended = jnp.dot(cotangent_seq, out_weight.T, preferred_element_type=jnp.float32).astype(jnp.bfloat16)
        grad_sum = grad_sum + jnp.dot(attended.T, cotangent_seq, preferred_element_type=jnp.float32)
        grad_queries, grad_keys, grad_values = pullback(d_attended)
        return (grad_sum, (projected, grad_queries, grad_keys, grad_values))
    grad_weight, outputs = lax.scan(per_sequence, jnp.zeros((HEADS * HD, DIM), jnp.float32), inputs)
    projected, grad_queries, grad_keys, grad_values = outputs
    return (projected.reshape(TOKENS, DIM), grad_queries.reshape(TOKENS, HEADS * HD), grad_keys.reshape(TOKENS, HEADS * HD), grad_values.reshape(TOKENS, HEADS * HD), grad_weight)
```

```python
import math

import jax
import jax.numpy as jnp
from jax import lax
from jax.sharding import PartitionSpec as P

F32 = jnp.float32
BF16 = jnp.bfloat16


def norm_rotate(heads_data, gain, patch_rows, patch_cols):
    center = heads_data - jnp.mean(heads_data, axis=-1, keepdims=True)
    spread = jnp.mean(center * center, axis=-1, keepdims=True)
    normed = center * lax.rsqrt(spread + 1e-06) * gain
    tokens_here, head_count, head_dim = normed.shape
    quarter = head_dim // 4
    frequency = 10000.0 ** (-jnp.arange(quarter, dtype=F32) / quarter)
    angles = jnp.stack(
        [
            patch_rows.astype(F32)[:, None] * frequency,
            patch_cols.astype(F32)[:, None] * frequency,
        ],
        axis=1,
    )
    cosine = jnp.cos(angles)[:, None]
    sine_table = jnp.sin(angles)[:, None]
    grouped = normed.reshape(tokens_here, head_count, 2, 2, quarter)
    lower_part = grouped[:, :, :, 0]
    upper_part = grouped[:, :, :, 1]
    rotated = jnp.stack(
        [
            lower_part * cosine - upper_part * sine_table,
            upper_part * cosine + lower_part * sine_table,
        ],
        axis=3,
    )
    return rotated.reshape(tokens_here, head_count, head_dim)


def stream(n, right, reach):
    pairs = []
    for z in range(n):
        for c in range(2):
            if right and z >= reach and z < n - 1:
                pairs.append((2 * z + c, 2 * (z + 1) + c))
            if not right and z <= n - 1 - reach and z > 0:
                pairs.append((2 * z + c, 2 * (z - 1) + c))
    return pairs


def gather_chain(shard, n, z):
    rights, lefts = [], []
    right = left = shard
    for k in range(n - 1):
        right = lax.ppermute(right, "dp", stream(n, True, k))
        left = lax.ppermute(left, "dp", stream(n, False, k))
        rights.append(right)
        lefts.append(left)
    line = jnp.stack(rights[::-1] + [shard] + lefts)
    return lax.dynamic_slice_in_dim(line, n - 1 - z, n, axis=0)


def scatter_chain(blocks, n, z):
    def pick(i):
        return lax.dynamic_index_in_dim(blocks, jnp.clip(i, 0, n - 1), 0, keepdims=False)

    right = left = None
    for d in range(n - 1, 0, -1):
        to_left, to_right = pick(z - d), pick(z + d)
        if left is not None:
            to_left = to_left + left.astype(F32)
            to_right = to_right + right.astype(F32)
        left_pairs = [p for p in stream(n, False, 0) if p[0] // 2 >= d]
        right_pairs = [p for p in stream(n, True, 0) if n - 1 - p[0] // 2 >= d]
        left = lax.ppermute(to_left.astype(BF16), "dp", left_pairs)
        right = lax.ppermute(to_right.astype(BF16), "dp", right_pairs)
    total = pick(z)
    if left is not None:
        total = total + left.astype(F32) + right.astype(F32)
    return total


def doubling(piece, bits, size, m):
    rows, cols = piece.shape
    axes = len(bits)
    held = piece.reshape((1,) * axes + (rows, cols))
    for bit in bits:
        other = lax.ppermute(held, "mp", [(i, i ^ (1 << bit)) for i in range(size)])
        mine_high = ((m >> bit) & 1) == 1
        axis = axes - 1 - bit
        held = jnp.concatenate(
            [jnp.where(mine_high, other, held), jnp.where(mine_high, held, other)], axis=axis
        )
    return held.reshape(size, rows, cols)


def halving(whole, bits, size, m):
    rows, cols = whole.shape[1:]
    axes = len(bits)
    held = whole.reshape((2,) * axes + (rows, cols))
    for bit in bits:
        axis = axes - 1 - bit
        low = lax.slice_in_dim(held, 0, 1, axis=axis)
        high = lax.slice_in_dim(held, 1, 2, axis=axis)
        mine_high = ((m >> bit) & 1) == 1
        send = jnp.where(mine_high, low, high).astype(BF16)
        keep = jnp.where(mine_high, high, low)
        got = lax.ppermute(send, "mp", [(i, i ^ (1 << bit)) for i in range(size)])
        held = keep.astype(F32) + got.astype(F32)
    return held.reshape(rows, cols)


def make_per_device(n_dp, n_mp):
    n = n_dp // 2
    bits = list(range(n_mp.bit_length() - 1))
    swap = [(i, i ^ 1) for i in range(n_dp)]

    def per_device(
        queries, keys, values, query_gain, key_gain, segments, patch_rows, patch_cols,
        image_counts, out_weight, cotangent,
    ):
        place = lax.axis_index("dp")
        z, c = place // 2, place % 2
        m = lax.axis_index("mp")
        seq, width = queries.shape
        hd = query_gain.shape[0]
        dim = out_weight.shape[1]
        rows = out_weight.shape[0]
        half = dim // 2

        w_own = gather_chain(out_weight, n, z)
        w_sib = lax.ppermute(w_own, "dp", swap)

        cot_a = doubling(cotangent[:, :half], bits, n_mp, m).reshape(seq, half)
        cot_b = doubling(cotangent[:, half:], bits[::-1], n_mp, m).reshape(seq, dim - half)
        cot = jnp.concatenate([cot_a, cot_b], axis=1)

        shaped = (seq, -1, hd)

        def rotate_q(x):
            return norm_rotate(x.astype(F32).reshape(shaped), query_gain, patch_rows, patch_cols)

        def rotate_k(x):
            return norm_rotate(x.astype(F32).reshape(shaped), key_gain, patch_rows, patch_cols)

        q_rot, q_pull = jax.vjp(rotate_q, queries)
        k_rot, k_pull = jax.vjp(rotate_k, keys)
        scale = 1.0 / math.sqrt(hd)
        scores = jnp.einsum(
            "shd,thd->hst", q_rot, k_rot, precision=lax.Precision.HIGHEST
        ) * scale
        allowed = (segments[:, None] == segments[None, :])[None]
        exp_scores = jnp.where(allowed, jnp.exp(scores), 0.0)
        probs = exp_scores / jnp.sum(exp_scores, axis=-1, keepdims=True)
        rounded = probs.astype(BF16)
        v_heads = values.reshape(shaped)
        live = (segments < image_counts[0])[:, None]
        context = jnp.einsum("hst,thd->shd", rounded, v_heads, preferred_element_type=F32)
        attended = jnp.where(live, context.reshape(seq, width), 0.0).astype(BF16)

        by_core = attended.reshape(seq, n, 2, rows)
        first, second = by_core[:, :, 0], by_core[:, :, 1]
        at_zero = c == 0
        att_own = jnp.where(at_zero, first, second).reshape(seq, n * rows)
        att_sib = jnp.where(at_zero, second, first).reshape(seq, n * rows)

        over_tokens = (((0,), (0,)), ((), ()))
        g_sib = lax.dot_general(att_sib, cot, over_tokens, preferred_element_type=F32)
        g_got = lax.ppermute(g_sib.astype(BF16), "dp", swap)
        g_own = lax.dot_general(att_own, cot, over_tokens, preferred_element_type=F32)
        g_chip = (g_own + g_got.astype(F32)).reshape(n, rows, dim)
        grad_weight = scatter_chain(g_chip, n, z)

        w_own2 = w_own.reshape(n * rows, dim)
        w_sib2 = w_sib.reshape(n * rows, dim)
        partial = jnp.dot(att_own, w_own2, preferred_element_type=F32) + jnp.dot(
            att_sib, w_sib2, preferred_element_type=F32
        )
        stacked = partial.astype(BF16).reshape(n_mp, seq // n_mp, dim)
        projected = jnp.concatenate(
            [
                halving(stacked[:, :, :half], bits, n_mp, m),
                halving(stacked[:, :, half:], bits[::-1], n_mp, m),
            ],
            axis=1,
        ).astype(BF16)

        transposed = (((1,), (1,)), ((), ()))
        d_own = lax.dot_general(cot, w_own2, transposed, preferred_element_type=F32).astype(BF16)
        d_sib = lax.dot_general(cot, w_sib2, transposed, preferred_element_type=F32).astype(BF16)
        d_own = d_own.reshape(seq, n, rows)
        d_sib = d_sib.reshape(seq, n, rows)
        d_att = jnp.stack(
            [jnp.where(at_zero, d_own, d_sib), jnp.where(at_zero, d_sib, d_own)], axis=2
        ).reshape(seq, width)
        d_ctx = jnp.where(live, d_att, jnp.zeros((), BF16)).reshape(shaped)
        grad_values = jnp.einsum(
            "hst,shd->thd", rounded, d_ctx, preferred_element_type=F32
        ).reshape(seq, width).astype(BF16)
        d_probs = jnp.einsum("shd,thd->hst", d_ctx, v_heads, preferred_element_type=F32)
        d_scores = probs * (d_probs - jnp.sum(d_probs * probs, axis=-1, keepdims=True)) * scale
        d_q = jnp.einsum("hst,thd->shd", d_scores, k_rot, precision=lax.Precision.HIGH)
        d_k = jnp.einsum("hst,shd->thd", d_scores, q_rot, precision=lax.Precision.HIGH)
        (grad_queries,) = q_pull(d_q)
        (grad_keys,) = k_pull(d_k)
        return projected, grad_queries, grad_keys, grad_values, grad_weight

    return per_device


def solution(mesh):
    return jax.shard_map(
        make_per_device(mesh.shape["dp"], mesh.shape["mp"]),
        mesh=mesh,
        in_specs=(
            P("dp", "mp"),
            P("dp", "mp"),
            P("dp", "mp"),
            P(),
            P(),
            P("dp"),
            P("dp"),
            P("dp"),
            P("dp"),
            P(("mp", "dp"), None),
            P(("dp", "mp"), None),
        ),
        out_specs=(
            P(("dp", "mp"), None),
            P("dp", "mp"),
            P("dp", "mp"),
            P("dp", "mp"),
            P(("mp", "dp"), None),
        ),
        check_vma=False,
    )
```

```python
import math

import jax
import jax.numpy as jnp
from jax import lax
from jax.sharding import PartitionSpec as P

F32 = jnp.float32
BF16 = jnp.bfloat16


def norm_rotate(heads_data, gain, patch_rows, patch_cols):
    center = heads_data - jnp.mean(heads_data, axis=-1, keepdims=True)
    spread = jnp.mean(center * center, axis=-1, keepdims=True)
    normed = center * lax.rsqrt(spread + 1e-06) * gain
    tokens_here, head_count, head_dim = normed.shape
    quarter = head_dim // 4
    frequency = 10000.0 ** (-jnp.arange(quarter, dtype=F32) / quarter)
    angles = jnp.stack(
        [
            patch_rows.astype(F32)[:, None] * frequency,
            patch_cols.astype(F32)[:, None] * frequency,
        ],
        axis=1,
    )
    cosine = jnp.cos(angles)[:, None]
    sine_table = jnp.sin(angles)[:, None]
    grouped = normed.reshape(tokens_here, head_count, 2, 2, quarter)
    lower_part = grouped[:, :, :, 0]
    upper_part = grouped[:, :, :, 1]
    rotated = jnp.stack(
        [
            lower_part * cosine - upper_part * sine_table,
            upper_part * cosine + lower_part * sine_table,
        ],
        axis=3,
    )
    return rotated.reshape(tokens_here, head_count, head_dim)


def stream(n, right, reach):
    pairs = []
    for z in range(n):
        for c in range(2):
            if right and z >= reach and z < n - 1:
                pairs.append((2 * z + c, 2 * (z + 1) + c))
            if not right and z <= n - 1 - reach and z > 0:
                pairs.append((2 * z + c, 2 * (z - 1) + c))
    return pairs


def gather_step(right, left, n, k):
    return (
        lax.ppermute(right, "dp", stream(n, True, k)),
        lax.ppermute(left, "dp", stream(n, False, k)),
    )


def gather_place(rights, shard, lefts, n, z):
    line = jnp.stack(rights[::-1] + [shard] + lefts)
    return lax.dynamic_slice_in_dim(line, n - 1 - z, n, axis=0)


def block_of(blocks, i):
    n = blocks.shape[0]
    return lax.dynamic_index_in_dim(blocks, jnp.clip(i, 0, n - 1), 0, keepdims=False)


def scatter_operands(blocks, got, n, z, d):
    right, left = block_of(blocks, z + d), block_of(blocks, z - d)
    if got is not None:
        right = right + got[0].astype(F32)
        left = left + got[1].astype(F32)
    return right.astype(BF16), left.astype(BF16)


def scatter_step(right, left, n, d):
    right_pairs = [p for p in stream(n, True, 0) if n - 1 - p[0] // 2 >= d]
    left_pairs = [p for p in stream(n, False, 0) if p[0] // 2 >= d]
    return lax.ppermute(right, "dp", right_pairs), lax.ppermute(left, "dp", left_pairs)


def doubling(piece, bits, size, m):
    rows, cols = piece.shape
    axes = len(bits)
    held = piece.reshape((1,) * axes + (rows, cols))
    for bit in bits:
        other = lax.ppermute(held, "mp", [(i, i ^ (1 << bit)) for i in range(size)])
        mine_high = ((m >> bit) & 1) == 1
        axis = axes - 1 - bit
        held = jnp.concatenate(
            [jnp.where(mine_high, other, held), jnp.where(mine_high, held, other)], axis=axis
        )
    return held.reshape(size, rows, cols)


def halving(whole, bits, size, m):
    rows, cols = whole.shape[1:]
    axes = len(bits)
    held = whole.reshape((2,) * axes + (rows, cols))
    for bit in bits:
        axis = axes - 1 - bit
        low = lax.slice_in_dim(held, 0, 1, axis=axis)
        high = lax.slice_in_dim(held, 1, 2, axis=axis)
        mine_high = ((m >> bit) & 1) == 1
        send = jnp.where(mine_high, low, high).astype(BF16)
        keep = jnp.where(mine_high, high, low)
        got = lax.ppermute(send, "mp", [(i, i ^ (1 << bit)) for i in range(size)])
        held = keep.astype(F32) + got.astype(F32)
    return held.reshape(rows, cols)


def make_per_device(n_dp, n_mp):
    n = n_dp // 2
    bits = list(range(n_mp.bit_length() - 1))
    swap = [(i, i ^ 1) for i in range(n_dp)]

    def per_device(
        queries, keys, values, query_gain, key_gain, segments, patch_rows, patch_cols,
        image_counts, out_weight, cotangent,
    ):
        place = lax.axis_index("dp")
        z, c = place // 2, place % 2
        m = lax.axis_index("mp")
        seq, width = queries.shape
        hd = query_gain.shape[0]
        dim = out_weight.shape[1]
        rows = out_weight.shape[0]
        half = dim // 2

        rights, lefts = [], []
        w_right = w_left = out_weight
        for k in range(max(n - 2, 0)):
            w_right, w_left = gather_step(w_right, w_left, n, k)
            rights.append(w_right)
            lefts.append(w_left)

        cot_a = doubling(cotangent[:, :half], bits, n_mp, m).reshape(seq, half)
        cot_b = doubling(cotangent[:, half:], bits[::-1], n_mp, m).reshape(seq, dim - half)
        cot = jnp.concatenate([cot_a, cot_b], axis=1)

        shaped = (seq, -1, hd)

        def rotate_q(x):
            return norm_rotate(x.astype(F32).reshape(shaped), query_gain, patch_rows, patch_cols)

        def rotate_k(x):
            return norm_rotate(x.astype(F32).reshape(shaped), key_gain, patch_rows, patch_cols)

        q_rot, q_pull = jax.vjp(rotate_q, queries)
        k_rot, k_pull = jax.vjp(rotate_k, keys)
        scale = 1.0 / math.sqrt(hd)
        scores = jnp.einsum(
            "shd,thd->hst", q_rot, k_rot, precision=lax.Precision.HIGHEST
        ) * scale
        allowed = (segments[:, None] == segments[None, :])[None]
        exp_scores = jnp.where(allowed, jnp.exp(scores), 0.0)
        probs = exp_scores / jnp.sum(exp_scores, axis=-1, keepdims=True)
        rounded = probs.astype(BF16)
        v_heads = values.reshape(shaped)
        live = (segments < image_counts[0])[:, None]
        context = jnp.einsum("hst,thd->shd", rounded, v_heads, preferred_element_type=F32)
        attended = jnp.where(live, context.reshape(seq, width), 0.0).astype(BF16)

        at_zero = c == 0

        def by_core(x):
            cuts = [x[:, i * rows : (i + 1) * rows] for i in range(2 * n)]
            own = [jnp.where(at_zero, cuts[2 * j], cuts[2 * j + 1]) for j in range(n)]
            sib = [jnp.where(at_zero, cuts[2 * j + 1], cuts[2 * j]) for j in range(n)]
            return jnp.concatenate(own, axis=1), jnp.concatenate(sib, axis=1)

        att_own, att_sib = by_core(attended)

        over_tokens = (((0,), (0,)), ((), ()))
        g_sib = lax.dot_general(att_sib, cot, over_tokens, preferred_element_type=F32)
        g_got = lax.ppermute(g_sib.astype(BF16), "dp", swap)
        g_own = lax.dot_general(att_own, cot, over_tokens, preferred_element_type=F32)
        g_chip = (g_own + g_got.astype(F32)).reshape(n, rows, dim)

        g_moved = None
        if n > 1:
            g_right, g_left = scatter_operands(g_chip, None, n, z, n - 1)
            w_right, w_left, g_right, g_left = lax.optimization_barrier(
                (w_right, w_left, g_right, g_left)
            )
            g_moved = scatter_step(g_right, g_left, n, n - 1)
            w_right, w_left = gather_step(w_right, w_left, n, n - 2)
            w_right, w_left, *g_moved = lax.optimization_barrier((w_right, w_left, *g_moved))
            rights.append(w_right)
            lefts.append(w_left)
        for d in range(n - 2, 1, -1):
            g_moved = scatter_step(*scatter_operands(g_chip, g_moved, n, z, d), n, d)
        w_own = gather_place(rights, out_weight, lefts, n, z)
        w_sib = lax.ppermute(w_own, "dp", swap)

        w_own2 = w_own.reshape(n * rows, dim)
        w_sib2 = w_sib.reshape(n * rows, dim)
        partial = jnp.dot(att_own, w_own2, preferred_element_type=F32) + jnp.dot(
            att_sib, w_sib2, preferred_element_type=F32
        )
        stacked = partial.astype(BF16).reshape(n_mp, seq // n_mp, dim)
        transposed = (((1,), (1,)), ((), ()))
        d_own = lax.dot_general(cot, w_own2, transposed, preferred_element_type=F32).astype(BF16)
        d_sib = lax.dot_general(cot, w_sib2, transposed, preferred_element_type=F32).astype(BF16)
        pieces = []
        for j in range(n):
            own, sib = (x[:, j * rows : (j + 1) * rows] for x in (d_own, d_sib))
            pieces += [jnp.where(at_zero, own, sib), jnp.where(at_zero, sib, own)]
        d_att = jnp.concatenate(pieces, axis=1)
        grad_weight = block_of(g_chip, z)
        if n > 1:
            if n > 2:
                *g_moved, d_att, stacked = lax.optimization_barrier((*g_moved, d_att, stacked))
                g_moved = scatter_step(*scatter_operands(g_chip, g_moved, n, z, 1), n, 1)
            grad_weight = grad_weight + g_moved[0].astype(F32) + g_moved[1].astype(F32)
        projected = jnp.concatenate(
            [
                halving(stacked[:, :, :half], bits, n_mp, m),
                halving(stacked[:, :, half:], bits[::-1], n_mp, m),
            ],
            axis=1,
        ).astype(BF16)

        d_ctx = jnp.where(live, d_att, jnp.zeros((), BF16)).reshape(shaped)
        grad_values = jnp.einsum(
            "hst,shd->thd", rounded, d_ctx, preferred_element_type=F32
        ).reshape(seq, width).astype(BF16)
        d_probs = jnp.einsum("shd,thd->hst", d_ctx, v_heads, preferred_element_type=F32)
        d_scores = probs * (d_probs - jnp.sum(d_probs * probs, axis=-1, keepdims=True)) * scale
        d_q = jnp.einsum("hst,thd->shd", d_scores, k_rot, precision=lax.Precision.HIGH)
        d_k = jnp.einsum("hst,shd->thd", d_scores, q_rot, precision=lax.Precision.HIGH)
        (grad_queries,) = q_pull(d_q)
        (grad_keys,) = k_pull(d_k)
        return projected, grad_queries, grad_keys, grad_values, grad_weight

    return per_device


def solution(mesh):
    return jax.shard_map(
        make_per_device(mesh.shape["dp"], mesh.shape["mp"]),
        mesh=mesh,
        in_specs=(
            P("dp", "mp"),
            P("dp", "mp"),
            P("dp", "mp"),
            P(),
            P(),
            P("dp"),
            P("dp"),
            P("dp"),
            P("dp"),
            P(("mp", "dp"), None),
            P(("dp", "mp"), None),
        ),
        out_specs=(
            P(("dp", "mp"), None),
            P("dp", "mp"),
            P("dp", "mp"),
            P("dp", "mp"),
            P(("mp", "dp"), None),
        ),
        check_vma=False,
    )
```

```python
import math

import jax
import jax.numpy as jnp
from jax import lax
from jax.sharding import PartitionSpec as P

F32 = jnp.float32
BF16 = jnp.bfloat16


def norm_rotate(heads_data, gain, patch_rows, patch_cols):
    center = heads_data - jnp.mean(heads_data, axis=-1, keepdims=True)
    spread = jnp.mean(center * center, axis=-1, keepdims=True)
    normed = center * lax.rsqrt(spread + 1e-06) * gain
    tokens_here, head_count, head_dim = normed.shape
    quarter = head_dim // 4
    frequency = 10000.0 ** (-jnp.arange(quarter, dtype=F32) / quarter)
    angles = jnp.stack(
        [
            patch_rows.astype(F32)[:, None] * frequency,
            patch_cols.astype(F32)[:, None] * frequency,
        ],
        axis=1,
    )
    cosine = jnp.cos(angles)[:, None]
    sine_table = jnp.sin(angles)[:, None]
    grouped = normed.reshape(tokens_here, head_count, 2, 2, quarter)
    lower_part = grouped[:, :, :, 0]
    upper_part = grouped[:, :, :, 1]
    rotated = jnp.stack(
        [
            lower_part * cosine - upper_part * sine_table,
            upper_part * cosine + lower_part * sine_table,
        ],
        axis=3,
    )
    return rotated.reshape(tokens_here, head_count, head_dim)


def stream(n, right, reach):
    pairs = []
    for z in range(n):
        for c in range(2):
            if right and z >= reach and z < n - 1:
                pairs.append((2 * z + c, 2 * (z + 1) + c))
            if not right and z <= n - 1 - reach and z > 0:
                pairs.append((2 * z + c, 2 * (z - 1) + c))
    return pairs


def gather_step(right, left, n, k):
    return (
        lax.ppermute(right, "dp", stream(n, True, k)),
        lax.ppermute(left, "dp", stream(n, False, k)),
    )


def gather_place(rights, shard, lefts, n, z):
    line = rights[::-1] + [shard] + lefts
    if n <= 4:
        slots = []
        for j in range(n):
            slot = line[n - 1 + j]
            for i in range(1, n):
                slot = jnp.where(z == i, line[n - 1 + j - i], slot)
            slots.append(slot)
        return jnp.stack(slots)
    line = jnp.stack(line)
    return lax.dynamic_slice_in_dim(line, n - 1 - z, n, axis=0)


def block_of(blocks, i):
    n = blocks.shape[0]
    return lax.dynamic_index_in_dim(blocks, jnp.clip(i, 0, n - 1), 0, keepdims=False)


def scatter_operands(blocks, got, n, z, d):
    right, left = block_of(blocks, z + d), block_of(blocks, z - d)
    if got is not None:
        right = right + got[0].astype(F32)
        left = left + got[1].astype(F32)
    return right.astype(BF16), left.astype(BF16)


def scatter_step(right, left, n, d):
    right_pairs = [p for p in stream(n, True, 0) if n - 1 - p[0] // 2 >= d]
    left_pairs = [p for p in stream(n, False, 0) if p[0] // 2 >= d]
    return lax.ppermute(right, "dp", right_pairs), lax.ppermute(left, "dp", left_pairs)


def doubling_step(held, bit, axes, size, m):
    other = lax.ppermute(held, "mp", [(i, i ^ (1 << bit)) for i in range(size)])
    mine_high = ((m >> bit) & 1) == 1
    return jnp.concatenate(
        [jnp.where(mine_high, other, held), jnp.where(mine_high, held, other)],
        axis=axes - 1 - bit,
    )


def halving_step(held, bit, axes, size, m):
    axis = axes - 1 - bit
    low = lax.slice_in_dim(held, 0, 1, axis=axis)
    high = lax.slice_in_dim(held, 1, 2, axis=axis)
    mine_high = ((m >> bit) & 1) == 1
    send = jnp.where(mine_high, low, high).astype(BF16)
    keep = jnp.where(mine_high, high, low)
    got = lax.ppermute(send, "mp", [(i, i ^ (1 << bit)) for i in range(size)])
    return keep, got


def make_per_device(n_dp, n_mp):
    n = n_dp // 2
    bits = list(range(n_mp.bit_length() - 1))
    swap = [(i, i ^ 1) for i in range(n_dp)]

    def per_device(
        queries, keys, values, query_gain, key_gain, segments, patch_rows, patch_cols,
        image_counts, out_weight, cotangent,
    ):
        place = lax.axis_index("dp")
        z, c = place // 2, place % 2
        m = lax.axis_index("mp")
        seq, width = queries.shape
        hd = query_gain.shape[0]
        dim = out_weight.shape[1]
        rows = out_weight.shape[0]
        half = dim // 2

        rights, lefts = [], []
        w_right = w_left = out_weight
        axes = len(bits)
        cots = [
            x.reshape((1,) * axes + x.shape) for x in (cotangent[:, :half], cotangent[:, half:])
        ]
        orders = (bits, bits[::-1])
        for step in range(max(axes, n - 2)):
            if step < axes:
                cots = [
                    doubling_step(x, order[step], axes, n_mp, m) for x, order in zip(cots, orders)
                ]
            if step < n - 2:
                w_right, w_left = gather_step(w_right, w_left, n, step)
                if step == 0:
                    w_right, w_left, *cots = lax.optimization_barrier((w_right, w_left, *cots))
                rights.append(w_right)
                lefts.append(w_left)
        cot = jnp.concatenate([x.reshape(seq, -1) for x in cots], axis=1)

        shaped = (seq, -1, hd)

        def rotate_q(x):
            return norm_rotate(x.astype(F32).reshape(shaped), query_gain, patch_rows, patch_cols)

        def rotate_k(x):
            return norm_rotate(x.astype(F32).reshape(shaped), key_gain, patch_rows, patch_cols)

        q_rot, q_pull = jax.vjp(rotate_q, queries)
        k_rot, k_pull = jax.vjp(rotate_k, keys)
        scale = 1.0 / math.sqrt(hd)
        scores = jnp.einsum(
            "shd,thd->hst", q_rot, k_rot, precision=lax.Precision.HIGHEST
        ) * scale
        allowed = (segments[:, None] == segments[None, :])[None]
        exp_scores = jnp.where(allowed, jnp.exp(scores), 0.0)
        probs = exp_scores / jnp.sum(exp_scores, axis=-1, keepdims=True)
        rounded = probs.astype(BF16)
        v_heads = values.reshape(shaped)
        live = (segments < image_counts[0])[:, None]
        context = jnp.einsum("hst,thd->shd", rounded, v_heads, preferred_element_type=F32)
        attended = jnp.where(live, context.reshape(seq, width), 0.0).astype(BF16)

        at_zero = c == 0

        def by_core(x):
            cuts = [x[:, i * rows : (i + 1) * rows] for i in range(2 * n)]
            own = [jnp.where(at_zero, cuts[2 * j], cuts[2 * j + 1]) for j in range(n)]
            sib = [jnp.where(at_zero, cuts[2 * j + 1], cuts[2 * j]) for j in range(n)]
            return jnp.concatenate(own, axis=1), jnp.concatenate(sib, axis=1)

        att_own, att_sib = by_core(attended)

        over_tokens = (((0,), (0,)), ((), ()))
        g_sib = lax.dot_general(att_sib, cot, over_tokens, preferred_element_type=F32)
        g_sib = g_sib.astype(BF16)
        w_right, w_left, g_sib = lax.optimization_barrier((w_right, w_left, g_sib))
        g_got = lax.ppermute(g_sib, "dp", swap)
        g_own = lax.dot_general(att_own, cot, over_tokens, preferred_element_type=F32)
        g_chip = (g_own + g_got.astype(F32)).reshape(n, rows, dim)

        g_moved = None
        if n > 1:
            g_right, g_left = scatter_operands(g_chip, None, n, z, n - 1)
            w_right, w_left, g_right, g_left = lax.optimization_barrier(
                (w_right, w_left, g_right, g_left)
            )
            g_moved = scatter_step(g_right, g_left, n, n - 1)
            w_right, w_left = gather_step(w_right, w_left, n, n - 2)
            w_right, w_left, *g_moved = lax.optimization_barrier((w_right, w_left, *g_moved))
            rights.append(w_right)
            lefts.append(w_left)
        for d in range(n - 2, 1, -1):
            sums = scatter_operands(g_chip, g_moved, n, z, d)
            *sums, rights[-1], lefts[-1] = lax.optimization_barrier(
                (*sums, rights[-1], lefts[-1])
            )
            g_moved = scatter_step(*sums, n, d)
        w_own = gather_place(rights, out_weight, lefts, n, z)
        w_sib = lax.ppermute(w_own, "dp", swap)

        w_own2 = w_own.reshape(n * rows, dim)
        w_sib2 = w_sib.reshape(n * rows, dim)
        partial = jnp.dot(att_own, w_own2, preferred_element_type=F32) + jnp.dot(
            att_sib, w_sib2, preferred_element_type=F32
        )
        stacked = partial.astype(BF16).reshape(n_mp, seq // n_mp, dim)
        transposed = (((1,), (1,)), ((), ()))
        d_own = lax.dot_general(cot, w_own2, transposed, preferred_element_type=F32).astype(BF16)
        d_sib = lax.dot_general(cot, w_sib2, transposed, preferred_element_type=F32).astype(BF16)
        pieces = []
        for j in range(n):
            own, sib = (x[:, j * rows : (j + 1) * rows] for x in (d_own, d_sib))
            pieces += [jnp.where(at_zero, own, sib), jnp.where(at_zero, sib, own)]
        d_att = jnp.concatenate(pieces, axis=1)
        outs = [
            x.reshape((2,) * axes + (seq // n_mp, -1))
            for x in (stacked[:, :, :half], stacked[:, :, half:])
        ]
        grad_weight = block_of(g_chip, z)
        if n > 1:
            if n > 2:
                sums = scatter_operands(g_chip, g_moved, n, z, 1)
                *sums, d_att, outs[0], outs[1] = lax.optimization_barrier((*sums, d_att, *outs))
                g_moved = scatter_step(*sums, n, 1)
            grad_weight = grad_weight + g_moved[0].astype(F32) + g_moved[1].astype(F32)

        def exchange(outs, step, tie):
            sent = [
                halving_step(x, order[step], axes, n_mp, m) for x, order in zip(outs, orders)
            ]
            *got, tie = lax.optimization_barrier((*(x[1] for x in sent), tie))
            sums = [keep.astype(F32) + x.astype(F32) for (keep, _), x in zip(sent, got)]
            return sums, tie

        d_ctx = jnp.where(live, d_att, jnp.zeros((), BF16)).reshape(shaped)
        grad_values = jnp.einsum(
            "hst,shd->thd", rounded, d_ctx, preferred_element_type=F32
        ).reshape(seq, width).astype(BF16)
        d_probs = jnp.einsum("shd,thd->hst", d_ctx, v_heads, preferred_element_type=F32)
        if axes > 0:
            outs, d_probs = exchange(outs, 0, d_probs)
        d_scores = probs * (d_probs - jnp.sum(d_probs * probs, axis=-1, keepdims=True)) * scale
        d_q = jnp.einsum("hst,thd->shd", d_scores, k_rot, precision=lax.Precision.HIGH)
        d_k = jnp.einsum("hst,shd->thd", d_scores, q_rot, precision=lax.Precision.HIGH)
        for step in range(1, axes):
            outs, d_k = exchange(outs, step, d_k)
        projected = jnp.concatenate([x.reshape(seq // n_mp, -1) for x in outs], axis=1).astype(BF16)
        (grad_queries,) = q_pull(d_q)
        (grad_keys,) = k_pull(d_k)
        return projected, grad_queries, grad_keys, grad_values, grad_weight

    return per_device


def solution(mesh):
    return jax.shard_map(
        make_per_device(mesh.shape["dp"], mesh.shape["mp"]),
        mesh=mesh,
        in_specs=(
            P("dp", "mp"),
            P("dp", "mp"),
            P("dp", "mp"),
            P(),
            P(),
            P("dp"),
            P("dp"),
            P("dp"),
            P("dp"),
            P(("mp", "dp"), None),
            P(("dp", "mp"), None),
        ),
        out_specs=(
            P(("dp", "mp"), None),
            P("dp", "mp"),
            P("dp", "mp"),
            P("dp", "mp"),
            P(("mp", "dp"), None),
        ),
        check_vma=False,
    )
```

```python
import math

import jax
import jax.numpy as jnp
from jax import lax
from jax.sharding import PartitionSpec as P

F32 = jnp.float32
BF16 = jnp.bfloat16


def norm_rotate(heads_data, gain, patch_rows, patch_cols):
    center = heads_data - jnp.mean(heads_data, axis=-1, keepdims=True)
    spread = jnp.mean(center * center, axis=-1, keepdims=True)
    normed = center * lax.rsqrt(spread + 1e-06) * gain
    tokens_here, head_count, head_dim = normed.shape
    quarter = head_dim // 4
    frequency = 10000.0 ** (-jnp.arange(quarter, dtype=F32) / quarter)
    angles = jnp.stack(
        [
            patch_rows.astype(F32)[:, None] * frequency,
            patch_cols.astype(F32)[:, None] * frequency,
        ],
        axis=1,
    )
    cosine = jnp.cos(angles)[:, None]
    sine_table = jnp.sin(angles)[:, None]
    grouped = normed.reshape(tokens_here, head_count, 2, 2, quarter)
    lower_part = grouped[:, :, :, 0]
    upper_part = grouped[:, :, :, 1]
    rotated = jnp.stack(
        [
            lower_part * cosine - upper_part * sine_table,
            upper_part * cosine + lower_part * sine_table,
        ],
        axis=3,
    )
    return rotated.reshape(tokens_here, head_count, head_dim)


def stream(n, right, reach):
    pairs = []
    for z in range(n):
        for c in range(2):
            if right and z >= reach and z < n - 1:
                pairs.append((2 * z + c, 2 * (z + 1) + c))
            if not right and z <= n - 1 - reach and z > 0:
                pairs.append((2 * z + c, 2 * (z - 1) + c))
    return pairs


def gather_step(right, left, n, k):
    return (
        lax.ppermute(right, "dp", stream(n, True, k)),
        lax.ppermute(left, "dp", stream(n, False, k)),
    )


def gather_place(rights, shard, lefts, n, z):
    line = rights[::-1] + [shard] + lefts
    if n <= 4:
        slots = []
        for j in range(n):
            slot = line[n - 1 + j]
            for i in range(1, n):
                slot = jnp.where(z == i, line[n - 1 + j - i], slot)
            slots.append(slot)
        return jnp.stack(slots)
    line = jnp.stack(line)
    return lax.dynamic_slice_in_dim(line, n - 1 - z, n, axis=0)


def block_of(blocks, i):
    n = blocks.shape[0]
    return lax.dynamic_index_in_dim(blocks, jnp.clip(i, 0, n - 1), 0, keepdims=False)


def scatter_operands(blocks, got, n, z, d):
    right, left = block_of(blocks, z + d), block_of(blocks, z - d)
    if got is not None:
        right = right + got[0].astype(F32)
        left = left + got[1].astype(F32)
    return right.astype(BF16), left.astype(BF16)


def scatter_step(right, left, n, d):
    right_pairs = [p for p in stream(n, True, 0) if n - 1 - p[0] // 2 >= d]
    left_pairs = [p for p in stream(n, False, 0) if p[0] // 2 >= d]
    return lax.ppermute(right, "dp", right_pairs), lax.ppermute(left, "dp", left_pairs)


def doubling_step(held, bit, axes, size, m):
    other = lax.ppermute(held, "mp", [(i, i ^ (1 << bit)) for i in range(size)])
    mine_high = ((m >> bit) & 1) == 1
    return jnp.concatenate(
        [jnp.where(mine_high, other, held), jnp.where(mine_high, held, other)],
        axis=axes - 1 - bit,
    )


def halving_step(held, bit, axes, size, m):
    axis = axes - 1 - bit
    low = lax.slice_in_dim(held, 0, 1, axis=axis)
    high = lax.slice_in_dim(held, 1, 2, axis=axis)
    mine_high = ((m >> bit) & 1) == 1
    send = jnp.where(mine_high, low, high).astype(BF16)
    keep = jnp.where(mine_high, high, low)
    got = lax.ppermute(send, "mp", [(i, i ^ (1 << bit)) for i in range(size)])
    return keep, got


def make_per_device(n_dp, n_mp):
    n = n_dp // 2
    bits = list(range(n_mp.bit_length() - 1))
    swap = [(i, i ^ 1) for i in range(n_dp)]

    def per_device(
        queries, keys, values, query_gain, key_gain, segments, patch_rows, patch_cols,
        image_counts, out_weight, cotangent,
    ):
        place = lax.axis_index("dp")
        z, c = place // 2, place % 2
        m = lax.axis_index("mp")
        seq, width = queries.shape
        hd = query_gain.shape[0]
        dim = out_weight.shape[1]
        rows = out_weight.shape[0]
        half = dim // 2

        rights, lefts = [], []
        w_right = w_left = out_weight
        axes = len(bits)
        cots = [
            x.reshape((1,) * axes + x.shape) for x in (cotangent[:, :half], cotangent[:, half:])
        ]
        orders = (bits, bits[::-1])
        for step in range(max(axes, n - 2)):
            if step < axes:
                cots = [
                    doubling_step(x, order[step], axes, n_mp, m) for x, order in zip(cots, orders)
                ]
            if step < n - 2:
                w_right, w_left = gather_step(w_right, w_left, n, step)
                if step == 0:
                    w_right, w_left, *cots = lax.optimization_barrier((w_right, w_left, *cots))
                rights.append(w_right)
                lefts.append(w_left)
        cot = jnp.concatenate([x.reshape(seq, -1) for x in cots], axis=1)

        shaped = (seq, -1, hd)

        def rotate_q(x):
            return norm_rotate(x.astype(F32).reshape(shaped), query_gain, patch_rows, patch_cols)

        def rotate_k(x):
            return norm_rotate(x.astype(F32).reshape(shaped), key_gain, patch_rows, patch_cols)

        q_rot, q_pull = jax.vjp(rotate_q, queries)
        k_rot, k_pull = jax.vjp(rotate_k, keys)
        scale = 1.0 / math.sqrt(hd)
        scores = jnp.einsum(
            "shd,thd->hst", q_rot, k_rot, precision=lax.Precision.HIGHEST
        ) * scale
        allowed = (segments[:, None] == segments[None, :])[None]
        exp_scores = jnp.where(allowed, jnp.exp(scores), 0.0)
        probs = exp_scores / jnp.sum(exp_scores, axis=-1, keepdims=True)
        rounded = probs.astype(BF16)
        v_heads = values.reshape(shaped)
        live = (segments < image_counts[0])[:, None]
        context = jnp.einsum("hst,thd->shd", rounded, v_heads, preferred_element_type=F32)
        attended = jnp.where(live, context.reshape(seq, width), 0.0).astype(BF16)

        at_zero = c == 0

        def by_core(x):
            cuts = [x[:, i * rows : (i + 1) * rows] for i in range(2 * n)]
            own = [jnp.where(at_zero, cuts[2 * j], cuts[2 * j + 1]) for j in range(n)]
            sib = [jnp.where(at_zero, cuts[2 * j + 1], cuts[2 * j]) for j in range(n)]
            return jnp.concatenate(own, axis=1), jnp.concatenate(sib, axis=1)

        att_own, att_sib = by_core(attended)

        over_tokens = (((0,), (0,)), ((), ()))
        g_sib = lax.dot_general(att_sib, cot, over_tokens, preferred_element_type=F32)
        g_sib = g_sib.astype(BF16)
        w_right, w_left, g_sib = lax.optimization_barrier((w_right, w_left, g_sib))
        g_got = lax.ppermute(g_sib, "dp", swap)
        g_own = lax.dot_general(att_own, cot, over_tokens, preferred_element_type=F32)
        g_chip = (g_own + g_got.astype(F32)).reshape(n, rows, dim)

        g_moved = None
        if n > 1:
            w_right, w_left = gather_step(w_right, w_left, n, n - 2)
            sums = scatter_operands(g_chip, None, n, z, n - 1)
            w_right, w_left, *sums = lax.optimization_barrier((w_right, w_left, *sums))
            g_moved = scatter_step(*sums, n, n - 1)
            rights.append(w_right)
            lefts.append(w_left)
        w_own = gather_place(rights, out_weight, lefts, n, z)
        w_sib = lax.ppermute(w_own, "dp", swap)
        for d in range(n - 2, 1, -1):
            sums = scatter_operands(g_chip, g_moved, n, z, d)
            *sums, w_sib = lax.optimization_barrier((*sums, w_sib))
            g_moved = scatter_step(*sums, n, d)

        w_own2 = w_own.reshape(n * rows, dim)
        w_sib2 = w_sib.reshape(n * rows, dim)
        partial = jnp.dot(att_own, w_own2, preferred_element_type=F32) + jnp.dot(
            att_sib, w_sib2, preferred_element_type=F32
        )
        stacked = partial.astype(BF16).reshape(n_mp, seq // n_mp, dim)
        transposed = (((1,), (1,)), ((), ()))
        d_own = lax.dot_general(cot, w_own2, transposed, preferred_element_type=F32).astype(BF16)
        d_sib = lax.dot_general(cot, w_sib2, transposed, preferred_element_type=F32).astype(BF16)
        pieces = []
        for j in range(n):
            own, sib = (x[:, j * rows : (j + 1) * rows] for x in (d_own, d_sib))
            pieces += [jnp.where(at_zero, own, sib), jnp.where(at_zero, sib, own)]
        d_att = jnp.concatenate(pieces, axis=1)
        outs = [
            x.reshape((2,) * axes + (seq // n_mp, -1))
            for x in (stacked[:, :, :half], stacked[:, :, half:])
        ]
        grad_weight = block_of(g_chip, z)
        if n > 1:
            if n > 2:
                sums = scatter_operands(g_chip, g_moved, n, z, 1)
                *sums, d_att, outs[0], outs[1] = lax.optimization_barrier((*sums, d_att, *outs))
                g_moved = scatter_step(*sums, n, 1)
            grad_weight = grad_weight + g_moved[0].astype(F32) + g_moved[1].astype(F32)

        def exchange(outs, step, tie):
            sent = [
                halving_step(x, order[step], axes, n_mp, m) for x, order in zip(outs, orders)
            ]
            *got, tie = lax.optimization_barrier((*(x[1] for x in sent), tie))
            sums = [keep.astype(F32) + x.astype(F32) for (keep, _), x in zip(sent, got)]
            return sums, tie

        d_ctx = jnp.where(live, d_att, jnp.zeros((), BF16)).reshape(shaped)
        grad_values = jnp.einsum(
            "hst,shd->thd", rounded, d_ctx, preferred_element_type=F32
        ).reshape(seq, width).astype(BF16)
        d_probs = jnp.einsum("shd,thd->hst", d_ctx, v_heads, preferred_element_type=F32)
        if axes > 0:
            outs, d_probs = exchange(outs, 0, d_probs)
        d_scores = probs * (d_probs - jnp.sum(d_probs * probs, axis=-1, keepdims=True)) * scale
        d_q = jnp.einsum("hst,thd->shd", d_scores, k_rot, precision=lax.Precision.HIGH)
        d_k = jnp.einsum("hst,shd->thd", d_scores, q_rot, precision=lax.Precision.HIGH)
        for step in range(1, axes):
            outs, d_k = exchange(outs, step, d_k)
        projected = jnp.concatenate([x.reshape(seq // n_mp, -1) for x in outs], axis=1).astype(BF16)
        (grad_queries,) = q_pull(d_q)
        (grad_keys,) = k_pull(d_k)
        return projected, grad_queries, grad_keys, grad_values, grad_weight

    return per_device


def solution(mesh):
    return jax.shard_map(
        make_per_device(mesh.shape["dp"], mesh.shape["mp"]),
        mesh=mesh,
        in_specs=(
            P("dp", "mp"),
            P("dp", "mp"),
            P("dp", "mp"),
            P(),
            P(),
            P("dp"),
            P("dp"),
            P("dp"),
            P("dp"),
            P(("mp", "dp"), None),
            P(("dp", "mp"), None),
        ),
        out_specs=(
            P(("dp", "mp"), None),
            P("dp", "mp"),
            P("dp", "mp"),
            P("dp", "mp"),
            P(("mp", "dp"), None),
        ),
        check_vma=False,
    )
```
